32 devices in a mesh: dp: 16 (over z, x, core), mp: 2 (over y).
Axes of the slice: x: 2, y: 2, z: 4, core: 2. Of those that a mesh axis runs over, the one named last changes fastest.
Arguments:
- features: bfloat16 [2048, 512], P('dp'), may hold values from -6 to 6
- w_in: bfloat16 [512, 512], P(None, 'mp'), may hold values from -0.25 to 0.25
- b_in: float32 [512], P('mp'), may hold values from -1 to 1
- w_out: bfloat16 [512, 128], P('mp'), may hold values from -0.25 to 0.25
- partner: int32 [2048], P('dp'), may hold values from 0 to 2047, as said below
- window: int32 [16], replicated, may hold values from 0 to 3
Outputs:
- row_loss: float32 [512], P('dp')
- grad_w_in: float32 [512, 512], P(None, 'mp')
- grad_b_in: float32 [512], P('mp')
- grad_w_out: float32 [512, 128], P('mp')
The draws below stay inside these ranges and needn't reach their ends.
Inputs may be any that keep to these rules, and one draw needn't show every extreme that they name: partner pairs the rows: partner[partner[i]] = i and partner[i] != i for every row i.
All inputs are finite; a program needn't handle non-finite values.
Results may differ from the reference program's by a relative error of at most 0.0027.
Values may be sent and summed in bfloat16 or wider, within the bound.
A program may use at most 64 MiB of HBM per device.

```python
import math
import jax
import jax.numpy as jnp
from jax import lax

C = 512
HID = 512
E = 128
B_DEV = 128
A_DEV = 32
ROWS = 2048
N_DP = 16


def pair_order(key):
    return jax.random.permutation(jax.random.fold_in(key, 7), ROWS).astype(jnp.int32)


def draw_partner(key, part):
    shuffled = pair_order(key)
    swapped = shuffled.reshape(-1, 2)[:, ::-1].reshape(-1)
    return jnp.zeros((ROWS,), jnp.int32).at[shuffled].set(swapped)


def draw_features(key, part):
    shuffled = pair_order(key)
    pair_of = jnp.zeros((ROWS,), jnp.int32).at[shuffled].set(jnp.arange(ROWS, dtype=jnp.int32) // 2)
    pair_count = ROWS // 2
    group_count = max(ROWS // 128, 1)
    member_of = jax.random.randint(jax.random.fold_in(key, 11), (pair_count,), 0, group_count)
    centers = jax.random.normal(jax.random.fold_in(key, 12), (group_count, C), jnp.float32)
    strength = jax.random.uniform(jax.random.fold_in(key, 13), (group_count,), jnp.float32, 0.15, 0.8)
    individual = jax.random.normal(jax.random.fold_in(key, 14), (pair_count, C), jnp.float32)
    jitter = jax.random.normal(jax.random.fold_in(key, 15), (ROWS, C), jnp.float32)
    weight_share = strength[member_of][:, None]
    pair_base = jnp.sqrt(weight_share) * centers[member_of] + jnp.sqrt(1.0 - weight_share) * individual
    crop_views = jnp.sqrt(0.91) * pair_base[pair_of] + 0.3 * jitter
    return jnp.clip(crop_views, -6.0, 6.0).astype(jnp.bfloat16)


def plant(array, stream_key, low, largest):
    shape = array.shape
    index_at = [jax.random.randint(jax.random.fold_in(stream_key, axis), (), 0, shape[axis]) for axis in range(len(shape))]
    array = array.at[tuple(index_at)].set(low)
    longest = shape.index(max(shape))
    index_at[longest] = (index_at[longest] + 1) % shape[longest]
    return array.at[tuple(index_at)].set(largest)


def steps_of(own_key, dims, cuts, smallest, high):
    def one(axis_at, parts):
        draws = jax.random.uniform(jax.random.fold_in(jax.random.fold_in(own_key, 6), axis_at), (parts,), jnp.float32, smallest / len(cuts), high / len(cuts))
        return jnp.repeat(jnp.exp(draws), dims[axis_at] // parts).reshape((-1,) + (1,) * (len(dims) - axis_at - 1))

    factor_of = one(*cuts[0])
    for cut in cuts[1:]:
        factor_of = factor_of * one(*cut)
    return factor_of


def scatter_about(key, dims, deviation, most, split=(), held_as=jnp.bfloat16):
    array = jax.random.normal(key, dims, jnp.float32) * deviation
    if len(split) > 0:
        array = steps_of(key, dims, split, -0.22, 0.18) * array
    return jnp.clip(array, min=-most, max=most).astype(held_as)


def setup_inputs(seed: int = 0) -> dict:
    arg_keys = jax.random.split(jax.random.key(seed), 7)
    features = draw_features(jax.random.fold_in(arg_keys[6], 71), 0)
    w_in = scatter_about(arg_keys[1], (C, HID), C ** -0.5, 0.25, ((1, 2),))
    b_in = jnp.clip(jax.random.uniform(arg_keys[2], (HID,), jnp.float32, -1.0, 1.0) * steps_of(arg_keys[2], (HID,), ((0, 2),), -0.4, 0.0), -1.0, 1.0)
    w_out = scatter_about(arg_keys[3], (HID, E), HID ** -0.5, 0.25, ((0, 2),))
    partner = draw_partner(jax.random.fold_in(arg_keys[6], 71), 0)
    window = plant(jax.random.randint(arg_keys[5], (N_DP,), 0, B_DEV // A_DEV), jax.random.fold_in(arg_keys[5], 1), 0, (B_DEV // A_DEV) - 1).astype(jnp.int32)
    return {"features": features, "w_in": w_in, "b_in": b_in, "w_out": w_out, "partner": partner, "window": window}


INV_TEMP = 10.0
SHIFT = 10.0
EPS = 1e-06

def reference(features, w_in, b_in, w_out, partner, window):
    pre = jnp.dot(features, w_in, preferred_element_type=jnp.float32) + b_in
    hidden = jax.nn.silu(pre).astype(jnp.bfloat16)
    proj = jnp.dot(hidden, w_out, preferred_element_type=jnp.float32)
    norm = jnp.sqrt(lax.optimization_barrier(jnp.sum(proj * proj, axis=1, keepdims=True)) + EPS)
    emb = (proj / norm).astype(jnp.bfloat16)
    total_rows = emb.shape[0]
    width = emb.shape[1]
    shard_count = window.shape[0]
    anchor_idx = ((jnp.arange(shard_count, dtype=jnp.int32) * B_DEV + window.astype(jnp.int32) * A_DEV)[:, None] + jnp.arange(A_DEV, dtype=jnp.int32)[None, :]).reshape(-1).astype(jnp.int32)
    anchor_total = anchor_idx.shape[0]
    anchor_emb = emb[anchor_idx]
    anchor_partner = partner[anchor_idx]
    blk = math.gcd(anchor_total, 512)
    count = anchor_total // blk
    col_ids = jnp.arange(total_rows, dtype=jnp.int32)
    emb_blocks = anchor_emb.reshape(count, blk, width)
    partner_blocks = anchor_partner.reshape(count, blk)
    id_blocks = anchor_idx.reshape(count, blk)

    def stats(carry, item):
        rows_emb, rows_partner, ids = item
        s = jnp.dot(rows_emb, emb.T, preferred_element_type=jnp.float32) * INV_TEMP
        ex = jnp.where(col_ids[None, :] == ids[:, None], 0.0, jnp.exp(s - SHIFT))
        hit = lax.optimization_barrier(jnp.sum(jnp.where(col_ids[None, :] == rows_partner[:, None], s, 0.0), axis=1))
        return (carry, (lax.optimization_barrier(jnp.sum(ex, axis=1)), hit))
    _, (total, hit) = lax.scan(stats, 0, (emb_blocks, partner_blocks, id_blocks))
    total = total.reshape(anchor_total)
    hit = hit.reshape(anchor_total)
    row_loss = jnp.log(total) + SHIFT - hit
    total_blocks = total.reshape(count, blk)

    def grads(acc, item):
        rows_emb, rows_partner, rows_total, ids = item
        s = jnp.dot(rows_emb, emb.T, preferred_element_type=jnp.float32) * INV_TEMP
        prob = jnp.where(col_ids[None, :] == ids[:, None], 0.0, jnp.exp(s - SHIFT) / rows_total[:, None])
        onehot = (col_ids[None, :] == rows_partner[:, None]).astype(jnp.float32)
        weights = (prob - onehot).astype(jnp.bfloat16)
        row_grad = jnp.dot(weights, emb, preferred_element_type=jnp.float32)
        acc = acc + lax.dot_general(weights, rows_emb, (((0,), (0,)), ((), ())), preferred_element_type=jnp.float32)
        return (acc, row_grad)
    col_grad, row_grad = lax.scan(grads, jnp.zeros((total_rows, width), jnp.float32), (emb_blocks, partner_blocks, total_blocks, id_blocks))
    row_full = jnp.zeros((total_rows, width), jnp.float32).at[anchor_idx].add(row_grad.reshape(anchor_total, width))
    grad_emb = (row_full + col_grad) * (INV_TEMP / anchor_total)
    unit = proj / norm
    grad_proj = ((grad_emb - unit * lax.optimization_barrier(jnp.sum(unit * grad_emb, axis=1, keepdims=True))) / norm).astype(jnp.bfloat16)
    grad_w_out = lax.dot_general(hidden, grad_proj, (((0,), (0,)), ((), ())), preferred_element_type=jnp.float32)
    grad_hidden = lax.dot_general(grad_proj, w_out, (((1,), (1,)), ((), ())), preferred_element_type=jnp.float32)
    sig = jax.nn.sigmoid(pre)
    grad_pre = (grad_hidden * sig * (1.0 + pre * (1.0 - sig))).astype(jnp.bfloat16)
    grad_w_in = lax.dot_general(features, grad_pre, (((0,), (0,)), ((), ())), preferred_element_type=jnp.float32)
    grad_b_in = lax.optimization_barrier(jnp.sum(grad_pre.astype(jnp.float32), axis=0))
    return (row_loss, grad_w_in, grad_b_in, grad_w_out)
```

```python
import functools

import jax
import jax.numpy as jnp
from jax import lax
from jax.experimental import pallas as pl
from jax.experimental.pallas import tpu as pltpu
from jax.sharding import PartitionSpec as P

A_DEV = 32
INV_TEMP = 10.0
SHIFT = 10.0
EPS = 1e-06
LOG2E = 1.4426950408889634
MESH = pl.DeviceIdType.MESH
F32 = jnp.float32
BF16 = jnp.bfloat16


def dot(a, b, dims=((1,), (0,))):
    return lax.dot_general(a, b, (dims, ((), ())), preferred_element_type=F32)


def kernel(
    n, rows, tile, a_chunk,
    f_ref, wi_ref, bi_ref, wo_ref, part_ref, win_ref,
    loss_ref, gwi_ref, gbi_ref, gwo_ref,
    feat, part, wi2, bi2, wo2, hid, dsil, proj, emb, anch, ids, ex, gemb,
    f_send, f_recv, p_send, p_recv, w_send, w_recv, loc_sem,
):
    me = lax.axis_index("dp")
    other = 1 - lax.axis_index("mp")
    total = n * rows
    embed = wo_ref.shape[1]
    anchors = n * A_DEV

    barrier = pltpu.get_barrier_semaphore()
    pl.semaphore_signal(barrier, inc=1, device_id={"mp": other}, device_id_type=MESH)

    def greet(r, _):
        peer = lax.rem(me + r, n)
        pl.semaphore_signal(barrier, inc=1, device_id={"dp": peer}, device_id_type=MESH)
        return 0

    lax.fori_loop(1, n, greet, 0)
    own_f = pltpu.make_async_copy(f_ref, feat.at[pl.ds(me * rows, rows)], loc_sem.at[0])
    own_p = pltpu.make_async_copy(part_ref, part.at[me], loc_sem.at[1])
    own_f.start()
    own_p.start()
    pl.semaphore_wait(barrier, n)

    w_copies = [
        pltpu.make_async_remote_copy(
            src_ref=src, dst_ref=dst, send_sem=w_send.at[i], recv_sem=w_recv.at[i],
            device_id={"mp": other}, device_id_type=MESH,
        )
        for i, (src, dst) in enumerate(((wi_ref, wi2), (wo_ref, wo2), (bi_ref, bi2)))
    ]
    for copy in w_copies:
        copy.start()

    def f_copy(slot, peer):
        return pltpu.make_async_remote_copy(
            src_ref=f_ref, dst_ref=feat.at[pl.ds(slot * rows, rows)],
            send_sem=f_send.at[peer], recv_sem=f_recv.at[slot],
            device_id={"dp": peer}, device_id_type=MESH,
        )

    def p_copy(slot, peer):
        return pltpu.make_async_remote_copy(
            src_ref=part_ref, dst_ref=part.at[slot],
            send_sem=p_send.at[peer], recv_sem=p_recv.at[slot],
            device_id={"dp": peer}, device_id_type=MESH,
        )

    def send(r, _):
        peer = lax.rem(me + r, n)
        f_copy(me, peer).start()
        p_copy(me, peer).start()
        return 0

    lax.fori_loop(1, n, send, 0)
    own_f.wait()
    own_p.wait()
    for copy in w_copies:
        copy.wait()

    def receive(r, _):
        peer = lax.rem(me + r, n)
        f_copy(peer, peer).wait_recv()
        p_copy(peer, peer).wait_recv()
        f_copy(me, peer).wait_send()
        p_copy(me, peer).wait_send()
        return 0

    lax.fori_loop(1, n, receive, 0)

    def embed_rows(start, size):
        at = pl.ds(start, size)
        x = feat[at, :]
        pre = dot(x, wi_ref[...]) + bi_ref[...]
        sig = jax.nn.sigmoid(pre)
        h = (pre * sig).astype(BF16)
        hid[at, :] = h
        if dsil is not None:
            dsil[at, :] = sig * (1.0 + pre * (1.0 - sig))
        pre2 = dot(x, wi2[...]) + bi2[...]
        h2 = (pre2 * jax.nn.sigmoid(pre2)).astype(BF16)
        y = dot(h, wo_ref[...]) + dot(h2, wo2[...])
        proj[at, :] = y
        inv = lax.rsqrt(jnp.sum(y * y, axis=1, keepdims=True) + EPS)
        emb[at, :] = (y * inv).astype(BF16)
        gemb[at, :] = jnp.zeros((size, embed), F32)

    def embed_tile(t, _):
        embed_rows(pl.multiple_of(t * tile, tile), tile)
        return 0

    lax.fori_loop(0, total // tile, embed_tile, 0)

    def window_of(b):
        return jnp.full((A_DEV, embed), win_ref[b], jnp.int32)

    def gather(b, _):
        win = window_of(b)
        picked = jnp.zeros((A_DEV, embed), F32)
        for w in range(rows // A_DEV):
            at = pl.ds(pl.multiple_of(b * rows + w * A_DEV, A_DEV), A_DEV)
            picked = jnp.where(win == w, emb[at, :].astype(F32), picked)
        at = pl.ds(pl.multiple_of(b * A_DEV, A_DEV), A_DEV)
        anch[at, :] = picked.astype(BF16)
        first = b * rows + win * A_DEV
        ids[at, :] = first + lax.broadcasted_iota(jnp.int32, (A_DEV, embed), 0)
        return 0

    lax.fori_loop(0, n, gather, 0)

    blocks = tile // rows
    reps = tile // embed

    def ids_of(base, size):
        return jnp.tile(ids[pl.ds(base, size), :], (1, reps))

    def col_ids(start, size):
        return start + lax.broadcasted_iota(jnp.int32, (size, tile), 1)

    def part_row(t):
        pieces = [part[t * blocks + i] for i in range(blocks)]
        return jnp.concatenate(pieces, axis=1) if blocks > 1 else pieces[0]

    mine = pl.multiple_of(me * A_DEV, A_DEV)
    own_anch = anch[pl.ds(mine, A_DEV), :]
    own_ids = ids_of(mine, A_DEV)

    def own_tile(t, carry):
        tot, hit = carry
        start = pl.multiple_of(t * tile, tile)
        d = dot(own_anch, emb[pl.ds(start, tile), :], ((1,), (1,)))
        e = jnp.where(
            col_ids(start, A_DEV) == own_ids, 0.0,
            jnp.exp2(d * (INV_TEMP * LOG2E) - SHIFT * LOG2E),
        )
        tot = tot + jnp.sum(e, axis=1, keepdims=True)
        h = jnp.where(part_row(t) == own_ids, d, 0.0)
        return (tot, hit + jnp.sum(h, axis=1, keepdims=True))

    zero = jnp.zeros((A_DEV, 1), F32)
    tot, hit = lax.fori_loop(0, total // tile, own_tile, (zero, zero))
    loss = jnp.log(tot) + SHIFT - hit * INV_TEMP
    r_iota = lax.broadcasted_iota(jnp.int32, (A_DEV, A_DEV), 0)
    c_iota = lax.broadcasted_iota(jnp.int32, (A_DEV, A_DEV), 1)
    loss_ref[...] = jnp.sum(jnp.where(r_iota == c_iota, loss, 0.0), axis=0, keepdims=True)

    def loss_chunk(k, _):
        base = pl.multiple_of(k * a_chunk, a_chunk)
        anc = anch[pl.ds(base, a_chunk), :]
        a_ids = ids_of(base, a_chunk)

        def soft(t, tot):
            start = pl.multiple_of(t * tile, tile)
            d = dot(anc, emb[pl.ds(start, tile), :], ((1,), (1,)))
            e = jnp.where(
                col_ids(start, a_chunk) == a_ids, 0.0,
                jnp.exp2(d * (INV_TEMP * LOG2E) - SHIFT * LOG2E),
            )
            ex[:, pl.ds(start, tile)] = e
            return tot + jnp.sum(e, axis=1, keepdims=True)

        tot = lax.fori_loop(0, total // tile, soft, jnp.zeros((a_chunk, 1), F32))
        inv = 1.0 / tot

        def back(t, acc):
            start = pl.multiple_of(t * tile, tile)
            at = pl.ds(start, tile)
            onehot = jnp.where(part_row(t) == a_ids, 1.0, 0.0)
            w = (ex[:, at] * inv - onehot).astype(BF16)
            gemb[at, :] += dot(w, anc, ((0,), (0,)))
            return acc + dot(w, emb[at, :])

        row = lax.fori_loop(0, total // tile, back, jnp.zeros((a_chunk, embed), F32))
        for i in range(a_chunk // A_DEV):
            b = k * (a_chunk // A_DEV) + i
            piece = row[i * A_DEV:(i + 1) * A_DEV, :]
            win = window_of(b)
            for w in range(rows // A_DEV):
                at = pl.ds(pl.multiple_of(b * rows + w * A_DEV, A_DEV), A_DEV)
                gemb[at, :] += jnp.where(win == w, piece, 0.0)
        return 0

    lax.fori_loop(0, anchors // a_chunk, loss_chunk, 0)

    gwi_ref[...] = jnp.zeros_like(gwi_ref)
    gwo_ref[...] = jnp.zeros_like(gwo_ref)
    gbi_ref[...] = jnp.zeros_like(gbi_ref)

    def grads(t, _):
        at = pl.ds(pl.multiple_of(t * tile, tile), tile)
        y = proj[at, :]
        inv = lax.rsqrt(jnp.sum(y * y, axis=1, keepdims=True) + EPS)
        unit = y * inv
        g = gemb[at, :] * (INV_TEMP / anchors)
        gp = ((g - unit * jnp.sum(unit * g, axis=1, keepdims=True)) * inv).astype(BF16)
        x = feat[at, :]
        h = hid[at, :]
        gwo_ref[...] += dot(h, gp, ((0,), (0,)))
        if dsil is not None:
            slope = dsil[at, :]
        else:
            pre = dot(x, wi_ref[...]) + bi_ref[...]
            sig = jax.nn.sigmoid(pre)
            slope = sig * (1.0 + pre * (1.0 - sig))
        gpre = (dot(gp, wo_ref[...], ((1,), (1,))) * slope).astype(BF16)
        gwi_ref[...] += dot(x, gpre, ((0,), (0,)))
        gbi_ref[...] += jnp.sum(gpre.astype(F32), axis=0, keepdims=True)
        return 0

    lax.fori_loop(0, total // tile, grads, 0)


def no_slope(n, rows, tile, a_chunk, *refs):
    return kernel(n, rows, tile, a_chunk, *refs[:16], None, *refs[16:])


def on_device(features, w_in, b_in, w_out, partner, window):
    n = lax.axis_size("dp")
    rows, chan = features.shape
    half = w_in.shape[1]
    embed = w_out.shape[1]
    total = n * rows
    tile = 4 * rows if n % 4 == 0 else rows
    anchors = n * A_DEV
    a_chunk = 256
    while a_chunk > A_DEV and (a_chunk * total > 2 ** 19 or anchors % a_chunk):
        a_chunk //= 2
    keep = total * half <= 2 ** 20
    scratch = [
        pltpu.VMEM((total, chan), BF16),
        pltpu.VMEM((n, 1, rows), jnp.int32),
        pltpu.VMEM((chan, half), BF16),
        pltpu.VMEM((1, half), F32),
        pltpu.VMEM((half, embed), BF16),
        pltpu.VMEM((total, half), BF16),
    ]
    if keep:
        scratch.append(pltpu.VMEM((total, half), F32))
    scratch += [
        pltpu.VMEM((total, embed), F32),
        pltpu.VMEM((total, embed), BF16),
        pltpu.VMEM((anchors, embed), BF16),
        pltpu.VMEM((anchors, embed), jnp.int32),
        pltpu.VMEM((a_chunk, total), F32),
        pltpu.VMEM((total, embed), F32),
        pltpu.SemaphoreType.DMA((n,)),
        pltpu.SemaphoreType.DMA((n,)),
        pltpu.SemaphoreType.DMA((n,)),
        pltpu.SemaphoreType.DMA((n,)),
        pltpu.SemaphoreType.DMA((3,)),
        pltpu.SemaphoreType.DMA((3,)),
        pltpu.SemaphoreType.DMA((2,)),
    ]
    vmem = pl.BlockSpec(memory_space=pltpu.VMEM)
    loss, gwi, gbi, gwo = pl.pallas_call(
        functools.partial(kernel if keep else no_slope, n, rows, tile, a_chunk),
        out_shape=(
            jax.ShapeDtypeStruct((1, A_DEV), F32),
            jax.ShapeDtypeStruct((chan, half), F32),
            jax.ShapeDtypeStruct((1, half), F32),
            jax.ShapeDtypeStruct((half, embed), F32),
        ),
        in_specs=[vmem] * 5 + [pl.BlockSpec(memory_space=pltpu.SMEM)],
        out_specs=(vmem,) * 4,
        scratch_shapes=scratch,
        compiler_params=pltpu.CompilerParams(
            collective_id=0, has_side_effects=True, vmem_limit_bytes=67043328
        ),
    )(features, w_in, b_in.reshape(1, half), w_out, partner.reshape(1, rows), window)
    return (loss.reshape(A_DEV), gwi, gbi.reshape(half), gwo)


def solution(mesh):
    return jax.shard_map(
        on_device,
        mesh=mesh,
        in_specs=(P("dp", None), P(None, "mp"), P("mp"), P("mp", None), P("dp"), P()),
        out_specs=(P("dp"), P(None, "mp"), P("mp"), P("mp", None)),
        check_vma=False,
    )
```

```python
import functools

import jax
import jax.numpy as jnp
from jax import lax
from jax.experimental import pallas as pl
from jax.experimental.pallas import tpu as pltpu
from jax.sharding import PartitionSpec as P

A_DEV = 32
INV_TEMP = 10.0
SHIFT = 10.0
EPS = 1e-06
LOG2E = 1.4426950408889634
MESH = pl.DeviceIdType.MESH
F32 = jnp.float32
BF16 = jnp.bfloat16


def dot(a, b, dims=((1,), (0,))):
    return lax.dot_general(a, b, (dims, ((), ())), preferred_element_type=F32)


def kernel(
    n, rows, tile, a_chunk,
    f_ref, wi_ref, bi_ref, wo_ref, part_ref, win_ref,
    loss_ref, gwi_ref, gbi_ref, gwo_ref,
    feat, part, wi2, bi2, wo2, hid, dsil, proj, emb, anch, ids, ex, gemb,
    send_sem, recv_sem, w_send, w_recv, loc_sem,
):
    me = lax.axis_index("dp")
    other = 1 - lax.axis_index("mp")
    total = n * rows
    embed = wo_ref.shape[1]
    anchors = n * A_DEV
    chan, half = wi_ref.shape

    depth = n // 4
    z = me // 4
    x_at = lax.rem(me // 2, 2)
    core = lax.rem(me, 2)
    links = (me - 4, me + 4, me + 2 - 4 * x_at, me + 1 - 2 * core)
    LEFT, RIGHT, ACROSS, SIBLING = range(4)
    has_left = z > 0
    has_right = z < depth - 1

    barrier = pltpu.get_barrier_semaphore()

    def greet(where):
        pl.semaphore_signal(barrier, inc=1, device_id=where, device_id_type=MESH)

    greet({"mp": other})
    greet({"dp": links[ACROSS]})
    greet({"dp": links[SIBLING]})

    @pl.when(has_left)
    def _():
        greet({"dp": links[LEFT]})

    @pl.when(has_right)
    def _():
        greet({"dp": links[RIGHT]})

    own_f = pltpu.make_async_copy(f_ref, feat.at[pl.ds(me * rows, rows)], loc_sem.at[0])
    own_p = pltpu.make_async_copy(part_ref, part.at[me], loc_sem.at[1])
    own_f.start()
    own_p.start()
    pl.semaphore_wait(
        barrier, 3 + jnp.where(has_left, 1, 0) + jnp.where(has_right, 1, 0)
    )

    cut = rows // 2

    def item(kind, slot, dest, own=False):
        if kind == 2:
            dst = part.at[slot]
            src = part_ref if own else dst
        else:
            dst = feat.at[pl.ds(slot * rows + kind * cut, cut)]
            src = f_ref.at[pl.ds(kind * cut, cut)] if own else dst
        return pltpu.make_async_remote_copy(
            src_ref=src, dst_ref=dst,
            send_sem=send_sem.at[(kind * 4 + dest) * n + slot],
            recv_sem=recv_sem.at[kind * n + slot],
            device_id={"dp": links[dest]}, device_id_type=MESH,
        )

    def got(kind, slot):
        item(kind, slot, SIBLING).wait_recv()

    wi_cut, wo_cut = chan // 2, half // 2

    def weights(base, device, relay, c):
        wi_at = pl.ds(c * wi_cut, wi_cut)
        wo_at = pl.ds(c * wo_cut, wo_cut)
        pairs = [
            ((wi2 if relay else wi_ref).at[wi_at], wi2.at[wi_at]),
            ((wo2 if relay else wo_ref).at[wo_at], wo2.at[wo_at]),
        ]
        if not relay:
            pairs.append((bi_ref, bi2))
        return [
            pltpu.make_async_remote_copy(
                src_ref=src, dst_ref=dst, send_sem=w_send.at[base + i],
                recv_sem=w_recv.at[base + i], device_id=device, device_id_type=MESH,
            )
            for i, (src, dst) in enumerate(pairs)
        ]

    w_out_copies = weights(0, {"mp": other}, False, core)
    w_relays = weights(3, {"dp": links[SIBLING]}, True, core)
    w_from_sib = weights(3, {"dp": links[SIBLING]}, True, 1 - core)

    def to(kind, slot, dest, start, own=False):
        copy = item(kind, slot, dest, own)
        if start:
            copy.start()
        else:
            copy.wait_send()

    def sides(kind, slot, start, own=False):
        @pl.when(has_left)
        def _():
            to(kind, slot, LEFT, start, own)

        @pl.when(has_right)
        def _():
            to(kind, slot, RIGHT, start, own)

    def own_sends(start):
        for kind in (0, 1, 2):
            sides(kind, me, start, True)
            to(kind, me, ACROSS, start, True)
        for kind in (0, 1, 2):
            to(kind, me, SIBLING, start, True)

    def first_step(start):
        slot = links[ACROSS]
        if start:
            got(1, slot)
        sides(1, slot, start)
        to(1, slot, SIBLING, start)
        for kind in (0, 2):
            if start:
                got(kind, slot)
            to(kind, slot, SIBLING, start)

    def from_side(slot, dest, more, start):
        twin = slot + links[ACROSS] - me
        for kind, source in ((0, slot), (1, slot), (1, twin), (2, slot)):
            if start:
                got(kind, source)

            @pl.when(more)
            def _():
                to(kind, source, dest, start)

            if source is slot and kind != 1:
                to(kind, source, ACROSS, start)
            to(kind, source, SIBLING, start)

    def from_across(slot, start):
        twin = slot + links[ACROSS] - me
        for kind in (0, 2):
            if start:
                got(kind, twin)
            to(kind, twin, SIBLING, start)

    def later_step(t, start):
        @pl.when(z - t >= 0)
        def _():
            from_side(me - 4 * t, RIGHT, has_right, start)

        @pl.when(z + t < depth)
        def _():
            from_side(me + 4 * t, LEFT, has_left, start)

        @pl.when(z - t >= 0)
        def _():
            from_across(me - 4 * t, start)

        @pl.when(z + t < depth)
        def _():
            from_across(me + 4 * t, start)

    own_sends(True)
    for copy in w_out_copies:
        copy.start()
    first_step(True)
    for copy in w_out_copies:
        copy.wait_recv()
    for copy in w_relays:
        copy.start()
    lax.fori_loop(1, depth, lambda t, _: (later_step(t, True), 0)[1], 0)
    own_f.wait()
    own_p.wait()
    for copy in w_from_sib:
        copy.wait_recv()

    def sibling_chip(q, _):
        slot = q * 2 + 1 - core
        for kind in (0, 1, 2):
            got(kind, slot)
        return 0

    lax.fori_loop(0, n // 2, sibling_chip, 0)

    def embed_rows(start, size):
        at = pl.ds(start, size)
        x = feat[at, :]
        pre = dot(x, wi_ref[...]) + bi_ref[...]
        sig = jax.nn.sigmoid(pre)
        h = (pre * sig).astype(BF16)
        hid[at, :] = h
        if dsil is not None:
            dsil[at, :] = sig * (1.0 + pre * (1.0 - sig))
        pre2 = dot(x, wi2[...]) + bi2[...]
        h2 = (pre2 * jax.nn.sigmoid(pre2)).astype(BF16)
        y = dot(h, wo_ref[...]) + dot(h2, wo2[...])
        proj[at, :] = y
        inv = lax.rsqrt(jnp.sum(y * y, axis=1, keepdims=True) + EPS)
        emb[at, :] = (y * inv).astype(BF16)
        gemb[at, :] = jnp.zeros((size, embed), F32)

    def embed_tile(t, _):
        embed_rows(pl.multiple_of(t * tile, tile), tile)
        return 0

    lax.fori_loop(0, total // tile, embed_tile, 0)

    def window_of(b):
        return jnp.full((A_DEV, embed), win_ref[b], jnp.int32)

    def gather(b, _):
        win = window_of(b)
        picked = jnp.zeros((A_DEV, embed), F32)
        for w in range(rows // A_DEV):
            at = pl.ds(pl.multiple_of(b * rows + w * A_DEV, A_DEV), A_DEV)
            picked = jnp.where(win == w, emb[at, :].astype(F32), picked)
        at = pl.ds(pl.multiple_of(b * A_DEV, A_DEV), A_DEV)
        anch[at, :] = picked.astype(BF16)
        first = b * rows + win * A_DEV
        ids[at, :] = first + lax.broadcasted_iota(jnp.int32, (A_DEV, embed), 0)
        return 0

    lax.fori_loop(0, n, gather, 0)

    blocks = tile // rows
    reps = tile // embed

    def ids_of(base, size):
        return jnp.tile(ids[pl.ds(base, size), :], (1, reps))

    def col_ids(start, size):
        return start + lax.broadcasted_iota(jnp.int32, (size, tile), 1)

    def part_row(t):
        pieces = [part[t * blocks + i] for i in range(blocks)]
        return jnp.concatenate(pieces, axis=1) if blocks > 1 else pieces[0]

    mine = pl.multiple_of(me * A_DEV, A_DEV)
    own_anch = anch[pl.ds(mine, A_DEV), :]
    own_ids = ids_of(mine, A_DEV)

    def own_tile(t, carry):
        tot, hit = carry
        start = pl.multiple_of(t * tile, tile)
        d = dot(own_anch, emb[pl.ds(start, tile), :], ((1,), (1,)))
        e = jnp.where(
            col_ids(start, A_DEV) == own_ids, 0.0,
            jnp.exp2(d * (INV_TEMP * LOG2E) - SHIFT * LOG2E),
        )
        tot = tot + jnp.sum(e, axis=1, keepdims=True)
        h = jnp.where(part_row(t) == own_ids, d, 0.0)
        return (tot, hit + jnp.sum(h, axis=1, keepdims=True))

    zero = jnp.zeros((A_DEV, 1), F32)
    tot, hit = lax.fori_loop(0, total // tile, own_tile, (zero, zero))
    loss = jnp.log(tot) + SHIFT - hit * INV_TEMP
    r_iota = lax.broadcasted_iota(jnp.int32, (A_DEV, A_DEV), 0)
    c_iota = lax.broadcasted_iota(jnp.int32, (A_DEV, A_DEV), 1)
    loss_ref[...] = jnp.sum(jnp.where(r_iota == c_iota, loss, 0.0), axis=0, keepdims=True)

    def loss_chunk(k, _):
        base = pl.multiple_of(k * a_chunk, a_chunk)
        anc = anch[pl.ds(base, a_chunk), :]
        a_ids = ids_of(base, a_chunk)

        def soft(t, tot):
            start = pl.multiple_of(t * tile, tile)
            d = dot(anc, emb[pl.ds(start, tile), :], ((1,), (1,)))
            e = jnp.where(
                col_ids(start, a_chunk) == a_ids, 0.0,
                jnp.exp2(d * (INV_TEMP * LOG2E) - SHIFT * LOG2E),
            )
            ex[:, pl.ds(start, tile)] = e
            return tot + jnp.sum(e, axis=1, keepdims=True)

        tot = lax.fori_loop(0, total // tile, soft, jnp.zeros((a_chunk, 1), F32))
        inv = 1.0 / tot

        def back(t, acc):
            start = pl.multiple_of(t * tile, tile)
            at = pl.ds(start, tile)
            onehot = jnp.where(part_row(t) == a_ids, 1.0, 0.0)
            w = (ex[:, at] * inv - onehot).astype(BF16)
            gemb[at, :] += dot(w, anc, ((0,), (0,)))
            return acc + dot(w, emb[at, :])

        row = lax.fori_loop(0, total // tile, back, jnp.zeros((a_chunk, embed), F32))
        for i in range(a_chunk // A_DEV):
            b = k * (a_chunk // A_DEV) + i
            piece = row[i * A_DEV:(i + 1) * A_DEV, :]
            win = window_of(b)
            for w in range(rows // A_DEV):
                at = pl.ds(pl.multiple_of(b * rows + w * A_DEV, A_DEV), A_DEV)
                gemb[at, :] += jnp.where(win == w, piece, 0.0)
        return 0

    lax.fori_loop(0, anchors // a_chunk, loss_chunk, 0)

    gwi_ref[...] = jnp.zeros_like(gwi_ref)
    gwo_ref[...] = jnp.zeros_like(gwo_ref)
    gbi_ref[...] = jnp.zeros_like(gbi_ref)

    def grads(t, _):
        at = pl.ds(pl.multiple_of(t * tile, tile), tile)
        y = proj[at, :]
        inv = lax.rsqrt(jnp.sum(y * y, axis=1, keepdims=True) + EPS)
        unit = y * inv
        g = gemb[at, :] * (INV_TEMP / anchors)
        gp = ((g - unit * jnp.sum(unit * g, axis=1, keepdims=True)) * inv).astype(BF16)
        x = feat[at, :]
        h = hid[at, :]
        gwo_ref[...] += dot(h, gp, ((0,), (0,)))
        if dsil is not None:
            slope = dsil[at, :]
        else:
            pre = dot(x, wi_ref[...]) + bi_ref[...]
            sig = jax.nn.sigmoid(pre)
            slope = sig * (1.0 + pre * (1.0 - sig))
        gpre = (dot(gp, wo_ref[...], ((1,), (1,))) * slope).astype(BF16)
        gwi_ref[...] += dot(x, gpre, ((0,), (0,)))
        gbi_ref[...] += jnp.sum(gpre.astype(F32), axis=0, keepdims=True)
        return 0

    lax.fori_loop(0, total // tile, grads, 0)

    own_sends(False)
    first_step(False)
    lax.fori_loop(1, depth, lambda t, _: (later_step(t, False), 0)[1], 0)
    for copy in w_out_copies + w_relays:
        copy.wait_send()


def no_slope(n, rows, tile, a_chunk, *refs):
    return kernel(n, rows, tile, a_chunk, *refs[:16], None, *refs[16:])


def on_device(features, w_in, b_in, w_out, partner, window):
    n = lax.axis_size("dp")
    rows, chan = features.shape
    half = w_in.shape[1]
    embed = w_out.shape[1]
    total = n * rows
    tile = 4 * rows if n % 4 == 0 else rows
    anchors = n * A_DEV
    a_chunk = 256
    while a_chunk > A_DEV and (a_chunk * total > 2 ** 19 or anchors % a_chunk):
        a_chunk //= 2
    keep = total * half <= 2 ** 20
    scratch = [
        pltpu.VMEM((total, chan), BF16),
        pltpu.VMEM((n, 1, rows), jnp.int32),
        pltpu.VMEM((chan, half), BF16),
        pltpu.VMEM((1, half), F32),
        pltpu.VMEM((half, embed), BF16),
        pltpu.VMEM((total, half), BF16),
    ]
    if keep:
        scratch.append(pltpu.VMEM((total, half), F32))
    scratch += [
        pltpu.VMEM((total, embed), F32),
        pltpu.VMEM((total, embed), BF16),
        pltpu.VMEM((anchors, embed), BF16),
        pltpu.VMEM((anchors, embed), jnp.int32),
        pltpu.VMEM((a_chunk, total), F32),
        pltpu.VMEM((total, embed), F32),
        pltpu.SemaphoreType.DMA((12 * n,)),
        pltpu.SemaphoreType.DMA((3 * n,)),
        pltpu.SemaphoreType.DMA((5,)),
        pltpu.SemaphoreType.DMA((5,)),
        pltpu.SemaphoreType.DMA((2,)),
    ]
    vmem = pl.BlockSpec(memory_space=pltpu.VMEM)
    loss, gwi, gbi, gwo = pl.pallas_call(
        functools.partial(kernel if keep else no_slope, n, rows, tile, a_chunk),
        out_shape=(
            jax.ShapeDtypeStruct((1, A_DEV), F32),
            jax.ShapeDtypeStruct((chan, half), F32),
            jax.ShapeDtypeStruct((1, half), F32),
            jax.ShapeDtypeStruct((half, embed), F32),
        ),
        in_specs=[vmem] * 5 + [pl.BlockSpec(memory_space=pltpu.SMEM)],
        out_specs=(vmem,) * 4,
        scratch_shapes=scratch,
        compiler_params=pltpu.CompilerParams(
            collective_id=0, has_side_effects=True, vmem_limit_bytes=67043328
        ),
    )(features, w_in, b_in.reshape(1, half), w_out, partner.reshape(1, rows), window)
    return (loss.reshape(A_DEV), gwi, gbi.reshape(half), gwo)


def solution(mesh):
    return jax.shard_map(
        on_device,
        mesh=mesh,
        in_specs=(P("dp", None), P(None, "mp"), P("mp"), P("mp", None), P("dp"), P()),
        out_specs=(P("dp"), P(None, "mp"), P("mp"), P("mp", None)),
        check_vma=False,
    )
```

```python
import functools

import jax
import jax.numpy as jnp
from jax import lax
from jax.experimental import pallas as pl
from jax.experimental.pallas import tpu as pltpu
from jax.sharding import PartitionSpec as P

A_DEV = 32
PAD = 16
INV_TEMP = 10.0
SHIFT = 10.0
EPS = 1e-06
LOG2E = 1.4426950408889634
MESH = pl.DeviceIdType.MESH
F32 = jnp.float32
BF16 = jnp.bfloat16


def dot(a, b, dims=((1,), (0,))):
    return lax.dot_general(a, b, (dims, ((), ())), preferred_element_type=F32)


def kernel(
    n, rows, tile, a_chunk,
    f_ref, wi_ref, bi_ref, wo_ref, part_ref, win_ref,
    loss_ref, gwi_ref, gbi_ref, gwo_ref,
    feat, part, wi2, bi2, wo2, hid, dsil, proj, emb, anch, ids, ex, gemb,
    send_sem, recv_sem, w_send, w_recv, loc_sem,
):
    me = lax.axis_index("dp")
    other = 1 - lax.axis_index("mp")
    total = n * rows
    embed = wo_ref.shape[1]
    anchors = n * A_DEV
    chan, half = wi_ref.shape

    depth = n // 4
    z = me // 4
    x_at = lax.rem(me // 2, 2)
    core = lax.rem(me, 2)
    links = (me - 4, me + 4, me + 2 - 4 * x_at, me + 1 - 2 * core)
    LEFT, RIGHT, ACROSS, SIBLING = range(4)
    has_left = z > 0
    has_right = z < depth - 1

    barrier = pltpu.get_barrier_semaphore()

    def greet(where):
        pl.semaphore_signal(barrier, inc=1, device_id=where, device_id_type=MESH)

    greet({"mp": other})
    greet({"dp": links[ACROSS]})
    greet({"dp": links[SIBLING]})

    @pl.when(has_left)
    def _():
        greet({"dp": links[LEFT]})

    @pl.when(has_right)
    def _():
        greet({"dp": links[RIGHT]})

    slot_rows = rows + PAD
    own_f = pltpu.make_async_copy(
        f_ref, feat.at[pl.ds(me * slot_rows, rows)], loc_sem.at[0]
    )
    own_f.start()
    ints = part_ref[...]
    pair = jnp.concatenate([ints // rows, lax.rem(ints, rows)], axis=1).astype(F32)
    feat[pl.ds(pl.multiple_of(me * slot_rows + rows, PAD), PAD), 0:2 * rows] = (
        jnp.broadcast_to(pair, (PAD, 2 * rows)).astype(BF16)
    )
    pl.semaphore_wait(
        barrier, 3 + jnp.where(has_left, 1, 0) + jnp.where(has_right, 1, 0)
    )

    def item(slot, dest):
        ref = feat.at[pl.ds(slot * slot_rows, slot_rows)]
        return pltpu.make_async_remote_copy(
            src_ref=ref, dst_ref=ref,
            send_sem=send_sem.at[dest * n + slot], recv_sem=recv_sem.at[slot],
            device_id={"dp": links[dest]}, device_id_type=MESH,
        )

    def got(slot):
        item(slot, SIBLING).wait_recv()

    wi_cut, wo_cut = chan // 2, half // 2

    def weights(base, device, relay, c):
        wi_at = pl.ds(c * wi_cut, wi_cut)
        wo_at = pl.ds(c * wo_cut, wo_cut)
        pairs = [
            ((wi2 if relay else wi_ref).at[wi_at], wi2.at[wi_at]),
            ((wo2 if relay else wo_ref).at[wo_at], wo2.at[wo_at]),
        ]
        if not relay:
            pairs.append((bi_ref, bi2))
        return [
            pltpu.make_async_remote_copy(
                src_ref=src, dst_ref=dst, send_sem=w_send.at[base + i],
                recv_sem=w_recv.at[base + i], device_id=device, device_id_type=MESH,
            )
            for i, (src, dst) in enumerate(pairs)
        ]

    w_out_copies = weights(0, {"mp": other}, False, core)
    w_relays = weights(3, {"dp": links[SIBLING]}, True, core)
    w_from_sib = weights(3, {"dp": links[SIBLING]}, True, 1 - core)

    def to(slot, dest, start):
        if start:
            item(slot, dest).start()
        else:
            item(slot, dest).wait_send()

    def sides(slot, start):
        @pl.when(has_left)
        def _():
            to(slot, LEFT, start)

        @pl.when(has_right)
        def _():
            to(slot, RIGHT, start)

    along = core == 0
    twin_off = links[ACROSS] - me

    def own_sends(start):
        to(me, ACROSS, start)
        sides(me, start)
        to(me, SIBLING, start)

    def first_step(start):
        slot = me + twin_off
        if start:
            got(slot)

        @pl.when(core == 1)
        def _():
            sides(slot, start)

        to(slot, SIBLING, start)

    def from_side(slot, dest, more, start):
        if start:
            got(slot)

        @pl.when(more)
        def _():
            to(slot, dest, start)

        @pl.when(along)
        def _():
            to(slot, ACROSS, start)

        to(slot, SIBLING, start)

    def twin_of(slot, dest, more, start):
        twin = slot + twin_off
        if start:
            got(twin)

        @pl.when(more & (core == 1))
        def _():
            to(twin, dest, start)

        to(twin, SIBLING, start)

    def later_step(t, start):
        for each in (from_side, twin_of):
            @pl.when(z - t >= 0)
            def _():
                each(me - 4 * t, RIGHT, has_right, start)

            @pl.when(z + t < depth)
            def _():
                each(me + 4 * t, LEFT, has_left, start)

    def feat_rows(first, count):
        pieces = [
            feat[pl.ds(pl.multiple_of((first + i) * slot_rows, PAD), rows), :]
            for i in range(count)
        ]
        return jnp.concatenate(pieces, axis=0)

    def embed_chip(chip):
        first = chip * 2
        at = pl.ds(pl.multiple_of(first * rows, 2 * rows), 2 * rows)
        x = feat_rows(first, 2)
        pre = dot(x, wi_ref[...]) + bi_ref[...]
        sig = jax.nn.sigmoid(pre)
        h = (pre * sig).astype(BF16)
        hid[at, :] = h
        if dsil is not None:
            dsil[at, :] = sig * (1.0 + pre * (1.0 - sig))
        pre2 = dot(x, wi2[...]) + bi2[...]
        h2 = (pre2 * jax.nn.sigmoid(pre2)).astype(BF16)
        y = dot(h, wo_ref[...]) + dot(h2, wo2[...])
        proj[at, :] = y
        inv = lax.rsqrt(jnp.sum(y * y, axis=1, keepdims=True) + EPS)
        emb[at, :] = (y * inv).astype(BF16)
        gemb[at, :] = jnp.zeros((2 * rows, embed), F32)

    own_f.wait()
    own_sends(True)
    for copy in w_out_copies:
        copy.start()
    first_step(True)
    for copy in w_out_copies:
        copy.wait_recv()
    for copy in w_relays:
        copy.start()

    def gather_step(t, _):
        @pl.when(t < depth)
        def _():
            later_step(t, True)

        @pl.when(t == 1)
        def _():
            for copy in w_from_sib:
                copy.wait_recv()

        def one(j, _):
            step = t - 1
            z_from = jnp.where(j < 2, z - step, z + step)
            chip = z_from * 2 + lax.rem(j, 2)
            ok = (z_from >= 0) & (z_from < depth) & ((j < 2) | (step > 0))

            @pl.when(ok)
            def _():
                got(chip * 2 + 1 - core)
                embed_chip(chip)

            return 0

        lax.fori_loop(0, 4, one, 0)
        return 0

    lax.fori_loop(1, depth + 1, gather_step, 0)

    def window_of(b):
        return jnp.full((A_DEV, embed), win_ref[b], jnp.int32)

    def gather(b, _):
        win = window_of(b)
        picked = jnp.zeros((A_DEV, embed), F32)
        for w in range(rows // A_DEV):
            at = pl.ds(pl.multiple_of(b * rows + w * A_DEV, A_DEV), A_DEV)
            picked = jnp.where(win == w, emb[at, :].astype(F32), picked)
        at = pl.ds(pl.multiple_of(b * A_DEV, A_DEV), A_DEV)
        anch[at, :] = picked.astype(BF16)
        first = b * rows + win * A_DEV
        ids[at, :] = first + lax.broadcasted_iota(jnp.int32, (A_DEV, embed), 0)
        return 0

    lax.fori_loop(0, n, gather, 0)

    blocks = tile // rows
    reps = tile // embed

    def ids_of(base, size):
        return jnp.tile(ids[pl.ds(base, size), :], (1, reps))

    def col_ids(start, size):
        return start + lax.broadcasted_iota(jnp.int32, (size, tile), 1)

    def unpack(t, _):
        r = feat[pl.ds(pl.multiple_of(t * slot_rows + rows, PAD), PAD), 0:2 * rows]
        v = r.astype(F32).astype(jnp.int32)
        part[t] = v[0:1, :rows] * rows + v[0:1, rows:]
        return 0

    lax.fori_loop(0, n, unpack, 0)

    def part_row(t):
        pieces = [part[t * blocks + i] for i in range(blocks)]
        return jnp.concatenate(pieces, axis=1) if blocks > 1 else pieces[0]

    mine = pl.multiple_of(me * A_DEV, A_DEV)
    own_anch = anch[pl.ds(mine, A_DEV), :]
    own_ids = ids_of(mine, A_DEV)

    def own_tile(t, carry):
        tot, hit = carry
        start = pl.multiple_of(t * tile, tile)
        d = dot(own_anch, emb[pl.ds(start, tile), :], ((1,), (1,)))
        e = jnp.where(
            col_ids(start, A_DEV) == own_ids, 0.0,
            jnp.exp2(d * (INV_TEMP * LOG2E) - SHIFT * LOG2E),
        )
        tot = tot + jnp.sum(e, axis=1, keepdims=True)
        h = jnp.where(part_row(t) == own_ids, d, 0.0)
        return (tot, hit + jnp.sum(h, axis=1, keepdims=True))

    zero = jnp.zeros((A_DEV, 1), F32)
    tot, hit = lax.fori_loop(0, total // tile, own_tile, (zero, zero))
    loss = jnp.log(tot) + SHIFT - hit * INV_TEMP
    r_iota = lax.broadcasted_iota(jnp.int32, (A_DEV, A_DEV), 0)
    c_iota = lax.broadcasted_iota(jnp.int32, (A_DEV, A_DEV), 1)
    loss_ref[...] = jnp.sum(jnp.where(r_iota == c_iota, loss, 0.0), axis=0, keepdims=True)

    def loss_chunk(k, _):
        base = pl.multiple_of(k * a_chunk, a_chunk)
        anc = anch[pl.ds(base, a_chunk), :]
        a_ids = ids_of(base, a_chunk)

        def soft(t, tot):
            start = pl.multiple_of(t * tile, tile)
            d = dot(anc, emb[pl.ds(start, tile), :], ((1,), (1,)))
            e = jnp.where(
                col_ids(start, a_chunk) == a_ids, 0.0,
                jnp.exp2(d * (INV_TEMP * LOG2E) - SHIFT * LOG2E),
            )
            ex[:, pl.ds(start, tile)] = e
            return tot + jnp.sum(e, axis=1, keepdims=True)

        tot = lax.fori_loop(0, total // tile, soft, jnp.zeros((a_chunk, 1), F32))
        inv = 1.0 / tot

        def back(t, acc):
            start = pl.multiple_of(t * tile, tile)
            at = pl.ds(start, tile)
            onehot = jnp.where(part_row(t) == a_ids, 1.0, 0.0)
            w = (ex[:, at] * inv - onehot).astype(BF16)
            gemb[at, :] += dot(w, anc, ((0,), (0,)))
            return acc + dot(w, emb[at, :])

        row = lax.fori_loop(0, total // tile, back, jnp.zeros((a_chunk, embed), F32))
        for i in range(a_chunk // A_DEV):
            b = k * (a_chunk // A_DEV) + i
            piece = row[i * A_DEV:(i + 1) * A_DEV, :]
            win = window_of(b)
            for w in range(rows // A_DEV):
                at = pl.ds(pl.multiple_of(b * rows + w * A_DEV, A_DEV), A_DEV)
                gemb[at, :] += jnp.where(win == w, piece, 0.0)
        return 0

    lax.fori_loop(0, anchors // a_chunk, loss_chunk, 0)

    gwi_ref[...] = jnp.zeros_like(gwi_ref)
    gwo_ref[...] = jnp.zeros_like(gwo_ref)
    gbi_ref[...] = jnp.zeros_like(gbi_ref)

    def grads(t, _):
        at = pl.ds(pl.multiple_of(t * tile, tile), tile)
        y = proj[at, :]
        inv = lax.rsqrt(jnp.sum(y * y, axis=1, keepdims=True) + EPS)
        unit = y * inv
        g = gemb[at, :] * (INV_TEMP / anchors)
        gp = ((g - unit * jnp.sum(unit * g, axis=1, keepdims=True)) * inv).astype(BF16)
        x = feat_rows(t * blocks, blocks)
        h = hid[at, :]
        gwo_ref[...] += dot(h, gp, ((0,), (0,)))
        if dsil is not None:
            slope = dsil[at, :]
        else:
            pre = dot(x, wi_ref[...]) + bi_ref[...]
            sig = jax.nn.sigmoid(pre)
            slope = sig * (1.0 + pre * (1.0 - sig))
        gpre = (dot(gp, wo_ref[...], ((1,), (1,))) * slope).astype(BF16)
        gwi_ref[...] += dot(x, gpre, ((0,), (0,)))
        gbi_ref[...] += jnp.sum(gpre.astype(F32), axis=0, keepdims=True)
        return 0

    lax.fori_loop(0, total // tile, grads, 0)

    own_sends(False)
    first_step(False)
    lax.fori_loop(1, depth, lambda t, _: (later_step(t, False), 0)[1], 0)
    for copy in w_out_copies + w_relays:
        copy.wait_send()


def no_slope(n, rows, tile, a_chunk, *refs):
    return kernel(n, rows, tile, a_chunk, *refs[:16], None, *refs[16:])


def on_device(features, w_in, b_in, w_out, partner, window):
    n = lax.axis_size("dp")
    rows, chan = features.shape
    half = w_in.shape[1]
    embed = w_out.shape[1]
    total = n * rows
    tile = 4 * rows if n % 4 == 0 else rows
    anchors = n * A_DEV
    a_chunk = 256
    while a_chunk > A_DEV and (a_chunk * total > 2 ** 19 or anchors % a_chunk):
        a_chunk //= 2
    keep = total * half <= 2 ** 20
    scratch = [
        pltpu.VMEM((n * (rows + PAD), chan), BF16),
        pltpu.VMEM((n, 1, rows), jnp.int32),
        pltpu.VMEM((chan, half), BF16),
        pltpu.VMEM((1, half), F32),
        pltpu.VMEM((half, embed), BF16),
        pltpu.VMEM((total, half), BF16),
    ]
    if keep:
        scratch.append(pltpu.VMEM((total, half), F32))
    scratch += [
        pltpu.VMEM((total, embed), F32),
        pltpu.VMEM((total, embed), BF16),
        pltpu.VMEM((anchors, embed), BF16),
        pltpu.VMEM((anchors, embed), jnp.int32),
        pltpu.VMEM((a_chunk, total), F32),
        pltpu.VMEM((total, embed), F32),
        pltpu.SemaphoreType.DMA((4 * n,)),
        pltpu.SemaphoreType.DMA((n,)),
        pltpu.SemaphoreType.DMA((5,)),
        pltpu.SemaphoreType.DMA((5,)),
        pltpu.SemaphoreType.DMA((1,)),
    ]
    vmem = pl.BlockSpec(memory_space=pltpu.VMEM)
    loss, gwi, gbi, gwo = pl.pallas_call(
        functools.partial(kernel if keep else no_slope, n, rows, tile, a_chunk),
        out_shape=(
            jax.ShapeDtypeStruct((1, A_DEV), F32),
            jax.ShapeDtypeStruct((chan, half), F32),
            jax.ShapeDtypeStruct((1, half), F32),
            jax.ShapeDtypeStruct((half, embed), F32),
        ),
        in_specs=[vmem] * 5 + [pl.BlockSpec(memory_space=pltpu.SMEM)],
        out_specs=(vmem,) * 4,
        scratch_shapes=scratch,
        compiler_params=pltpu.CompilerParams(
            collective_id=0, has_side_effects=True, vmem_limit_bytes=67043328
        ),
    )(features, w_in, b_in.reshape(1, half), w_out, partner.reshape(1, rows), window)
    return (loss.reshape(A_DEV), gwi, gbi.reshape(half), gwo)


def solution(mesh):
    return jax.shard_map(
        on_device,
        mesh=mesh,
        in_specs=(P("dp", None), P(None, "mp"), P("mp"), P("mp", None), P("dp"), P()),
        out_specs=(P("dp"), P(None, "mp"), P("mp"), P("mp", None)),
        check_vma=False,
    )
```

```python
import functools

import jax
import jax.numpy as jnp
from jax import lax
from jax.experimental import pallas as pl
from jax.experimental.pallas import tpu as pltpu
from jax.sharding import PartitionSpec as P

A_DEV = 32
PAD = 16
INV_TEMP = 10.0
SHIFT = 10.0
EPS = 1e-06
LOG2E = 1.4426950408889634
MESH = pl.DeviceIdType.MESH
F32 = jnp.float32
BF16 = jnp.bfloat16


def dot(a, b, dims=((1,), (0,))):
    return lax.dot_general(a, b, (dims, ((), ())), preferred_element_type=F32)


def kernel(
    n, rows, tile, a_chunk,
    f_ref, wi_ref, bi_ref, wo_ref, part_ref, win_ref,
    loss_ref, gwi_ref, gbi_ref, gwo_ref,
    feat, part, wi2, bi2, wo2, hid, dsil, proj, emb, anch, ids, ex, gemb,
    send_sem, recv_sem, w_send, w_recv, loc_sem,
):
    me = lax.axis_index("dp")
    other = 1 - lax.axis_index("mp")
    total = n * rows
    embed = wo_ref.shape[1]
    anchors = n * A_DEV
    chan, half = wi_ref.shape

    depth = n // 4
    z = me // 4
    x_at = lax.rem(me // 2, 2)
    core = lax.rem(me, 2)
    links = (me - 4, me + 4, me + 2 - 4 * x_at, me + 1 - 2 * core)
    LEFT, RIGHT, ACROSS, SIBLING = range(4)
    has_left = z > 0
    has_right = z < depth - 1

    barrier = pltpu.get_barrier_semaphore()

    def greet(where):
        pl.semaphore_signal(barrier, inc=1, device_id=where, device_id_type=MESH)

    greet({"mp": other})
    greet({"dp": links[ACROSS]})
    greet({"dp": links[SIBLING]})

    @pl.when(has_left)
    def _():
        greet({"dp": links[LEFT]})

    @pl.when(has_right)
    def _():
        greet({"dp": links[RIGHT]})

    slot_rows = rows + PAD
    own_f = pltpu.make_async_copy(
        f_ref, feat.at[pl.ds(me * slot_rows, rows)], loc_sem.at[0]
    )
    own_f.start()
    ints = part_ref[...]
    pair = jnp.concatenate([ints // rows, lax.rem(ints, rows)], axis=1).astype(F32)
    feat[pl.ds(pl.multiple_of(me * slot_rows + rows, PAD), PAD), 0:2 * rows] = (
        jnp.broadcast_to(pair, (PAD, 2 * rows)).astype(BF16)
    )
    pl.semaphore_wait(
        barrier, 3 + jnp.where(has_left, 1, 0) + jnp.where(has_right, 1, 0)
    )

    def item(slot, dest):
        ref = feat.at[pl.ds(slot * slot_rows, slot_rows)]
        return pltpu.make_async_remote_copy(
            src_ref=ref, dst_ref=ref,
            send_sem=send_sem.at[dest * n + slot], recv_sem=recv_sem.at[slot],
            device_id={"dp": links[dest]}, device_id_type=MESH,
        )

    def got(slot):
        item(slot, SIBLING).wait_recv()

    wi_cut, wo_cut = chan // 2, half // 2

    def weights(base, device, relay, c):
        wi_at = pl.ds(c * wi_cut, wi_cut)
        wo_at = pl.ds(c * wo_cut, wo_cut)
        pairs = [
            ((wi2 if relay else wi_ref).at[wi_at], wi2.at[wi_at]),
            ((wo2 if relay else wo_ref).at[wo_at], wo2.at[wo_at]),
        ]
        if not relay:
            pairs.append((bi_ref, bi2))
        return [
            pltpu.make_async_remote_copy(
                src_ref=src, dst_ref=dst, send_sem=w_send.at[base + i],
                recv_sem=w_recv.at[base + i], device_id=device, device_id_type=MESH,
            )
            for i, (src, dst) in enumerate(pairs)
        ]

    w_out_copies = weights(0, {"mp": other}, False, core)
    w_relays = weights(3, {"dp": links[SIBLING]}, True, core)
    w_from_sib = weights(3, {"dp": links[SIBLING]}, True, 1 - core)

    def to(slot, dest, start):
        if start:
            item(slot, dest).start()
        else:
            item(slot, dest).wait_send()

    def sides(slot, start):
        @pl.when(has_left)
        def _():
            to(slot, LEFT, start)

        @pl.when(has_right)
        def _():
            to(slot, RIGHT, start)

    along = core == 0
    twin_off = links[ACROSS] - me

    def own_sends(start):
        to(me, ACROSS, start)
        sides(me, start)
        to(me, SIBLING, start)

    def first_step(start):
        slot = me + twin_off
        if start:
            got(slot)

        @pl.when(core == 1)
        def _():
            sides(slot, start)

        to(slot, SIBLING, start)

    def from_side(slot, dest, more, start):
        if start:
            got(slot)

        @pl.when(more)
        def _():
            to(slot, dest, start)

        @pl.when(along)
        def _():
            to(slot, ACROSS, start)

        to(slot, SIBLING, start)

    def twin_of(slot, dest, more, start):
        twin = slot + twin_off
        if start:
            got(twin)

        @pl.when(more & (core == 1))
        def _():
            to(twin, dest, start)

        to(twin, SIBLING, start)

    def later_step(t, start):
        for each in (from_side, twin_of):
            @pl.when(z - t >= 0)
            def _():
                each(me - 4 * t, RIGHT, has_right, start)

            @pl.when(z + t < depth)
            def _():
                each(me + 4 * t, LEFT, has_left, start)

    def feat_rows(first, count):
        pieces = [
            feat[pl.ds(pl.multiple_of((first + i) * slot_rows, PAD), rows), :]
            for i in range(count)
        ]
        return jnp.concatenate(pieces, axis=0)

    def embed_chip(chip):
        first = chip * 2
        at = pl.ds(pl.multiple_of(first * rows, 2 * rows), 2 * rows)
        x = feat_rows(first, 2)
        pre = dot(x, wi_ref[...]) + bi_ref[...]
        sig = jax.nn.sigmoid(pre)
        h = (pre * sig).astype(BF16)
        hid[at, :] = h
        if dsil is not None:
            dsil[at, :] = sig * (1.0 + pre * (1.0 - sig))
        pre2 = dot(x, wi2[...]) + bi2[...]
        h2 = (pre2 * jax.nn.sigmoid(pre2)).astype(BF16)
        y = dot(h, wo_ref[...]) + dot(h2, wo2[...])
        proj[at, :] = y
        inv = lax.rsqrt(jnp.sum(y * y, axis=1, keepdims=True) + EPS)
        emb[at, :] = (y * inv).astype(BF16)
        gemb[at, :] = jnp.zeros((2 * rows, embed), F32)

    own_f.wait()
    own_sends(True)
    for copy in w_out_copies:
        copy.start()
    first_step(True)
    for copy in w_out_copies:
        copy.wait_recv()
    for copy in w_relays:
        copy.start()

    def gather_step(t, _):
        @pl.when(t < depth)
        def _():
            later_step(t, True)

        @pl.when(t == 1)
        def _():
            for copy in w_from_sib:
                copy.wait_recv()

        def one(j, _):
            step = t - 1
            z_from = jnp.where(j < 2, z - step, z + step)
            chip = z_from * 2 + lax.rem(j, 2)
            ok = (z_from >= 0) & (z_from < depth) & ((j < 2) | (step > 0))

            @pl.when(ok)
            def _():
                got(chip * 2 + 1 - core)
                embed_chip(chip)

            return 0

        lax.fori_loop(0, 4, one, 0)
        return 0

    lax.fori_loop(1, depth + 1, gather_step, 0)

    def window_of(b):
        return jnp.full((A_DEV, embed), win_ref[b], jnp.int32)

    def gather(b, _):
        win = window_of(b)
        picked = jnp.zeros((A_DEV, embed), F32)
        for w in range(rows // A_DEV):
            at = pl.ds(pl.multiple_of(b * rows + w * A_DEV, A_DEV), A_DEV)
            picked = jnp.where(win == w, emb[at, :].astype(F32), picked)
        at = pl.ds(pl.multiple_of(b * A_DEV, A_DEV), A_DEV)
        anch[at, :] = picked.astype(BF16)
        first = b * rows + win * A_DEV
        ids[at, :] = first + lax.broadcasted_iota(jnp.int32, (A_DEV, embed), 0)
        return 0

    lax.fori_loop(0, n, gather, 0)

    blocks = tile // rows
    reps = tile // embed

    def ids_of(base, size):
        return jnp.tile(ids[pl.ds(base, size), :], (1, reps))

    def col_ids(start, size):
        return start + lax.broadcasted_iota(jnp.int32, (size, tile), 1)

    def unpack(t, _):
        r = feat[pl.ds(pl.multiple_of(t * slot_rows + rows, PAD), PAD), 0:2 * rows]
        v = r.astype(F32).astype(jnp.int32)
        part[t] = v[0:1, :rows] * rows + v[0:1, rows:]
        return 0

    lax.fori_loop(0, n, unpack, 0)

    def part_row(t):
        pieces = [part[t * blocks + i] for i in range(blocks)]
        return jnp.concatenate(pieces, axis=1) if blocks > 1 else pieces[0]

    mine = pl.multiple_of(me * A_DEV, A_DEV)
    own_anch = anch[pl.ds(mine, A_DEV), :]
    own_ids = ids_of(mine, A_DEV)

    def own_tile(t, carry):
        tot, hit = carry
        start = pl.multiple_of(t * tile, tile)
        d = dot(own_anch, emb[pl.ds(start, tile), :], ((1,), (1,)))
        e = jnp.where(
            col_ids(start, A_DEV) == own_ids, 0.0,
            jnp.exp2(d * (INV_TEMP * LOG2E) - SHIFT * LOG2E),
        )
        tot = tot + jnp.sum(e, axis=1, keepdims=True)
        h = jnp.where(part_row(t) == own_ids, d, 0.0)
        return (tot, hit + jnp.sum(h, axis=1, keepdims=True))

    zero = jnp.zeros((A_DEV, 1), F32)
    tot, hit = lax.fori_loop(0, total // tile, own_tile, (zero, zero))
    loss = jnp.log(tot) + SHIFT - hit * INV_TEMP
    r_iota = lax.broadcasted_iota(jnp.int32, (A_DEV, A_DEV), 0)
    c_iota = lax.broadcasted_iota(jnp.int32, (A_DEV, A_DEV), 1)
    loss_ref[...] = jnp.sum(jnp.where(r_iota == c_iota, loss, 0.0), axis=0, keepdims=True)

    def loss_chunk(k, _):
        base = pl.multiple_of(k * a_chunk, a_chunk)
        anc = anch[pl.ds(base, a_chunk), :]
        a_ids = ids_of(base, a_chunk)

        def soft(t, tot):
            start = pl.multiple_of(t * tile, tile)
            d = dot(anc, emb[pl.ds(start, tile), :], ((1,), (1,)))
            e = jnp.where(
                col_ids(start, a_chunk) == a_ids, 0.0,
                jnp.exp2(d * (INV_TEMP * LOG2E) - SHIFT * LOG2E),
            )
            ex[:, pl.ds(start, tile)] = e
            return tot + jnp.sum(e, axis=1, keepdims=True)

        tot = lax.fori_loop(0, total // tile, soft, jnp.zeros((a_chunk, 1), F32))
        inv = 1.0 / tot

        def back(t, acc):
            start = pl.multiple_of(t * tile, tile)
            at = pl.ds(start, tile)
            onehot = jnp.where(part_row(t) == a_ids, 1.0, 0.0)
            w = (ex[:, at] * inv - onehot).astype(BF16)
            gemb[at, :] += dot(w, anc, ((0,), (0,)))
            return acc + dot(w, emb[at, :])

        row = lax.fori_loop(0, total // tile, back, jnp.zeros((a_chunk, embed), F32))
        for i in range(a_chunk // A_DEV):
            b = k * (a_chunk // A_DEV) + i
            piece = row[i * A_DEV:(i + 1) * A_DEV, :]
            win = window_of(b)
            for w in range(rows // A_DEV):
                at = pl.ds(pl.multiple_of(b * rows + w * A_DEV, A_DEV), A_DEV)
                gemb[at, :] += jnp.where(win == w, piece, 0.0)
        return 0

    lax.fori_loop(0, anchors // a_chunk, loss_chunk, 0)

    gwi_ref[...] = jnp.zeros_like(gwi_ref)
    gwo_ref[...] = jnp.zeros_like(gwo_ref)
    gbi_ref[...] = jnp.zeros_like(gbi_ref)

    def grads(t, _):
        at = pl.ds(pl.multiple_of(t * tile, tile), tile)
        y = proj[at, :]
        inv = lax.rsqrt(jnp.sum(y * y, axis=1, keepdims=True) + EPS)
        unit = y * inv
        g = gemb[at, :] * (INV_TEMP / anchors)
        gp = ((g - unit * jnp.sum(unit * g, axis=1, keepdims=True)) * inv).astype(BF16)
        x = feat_rows(t * blocks, blocks)
        h = hid[at, :]
        gwo_ref[...] += dot(h, gp, ((0,), (0,)))
        if dsil is not None:
            slope = dsil[at, :]
        else:
            pre = dot(x, wi_ref[...]) + bi_ref[...]
            sig = jax.nn.sigmoid(pre)
            slope = sig * (1.0 + pre * (1.0 - sig))
        gpre = (dot(gp, wo_ref[...], ((1,), (1,))) * slope).astype(BF16)
        gwi_ref[...] += dot(x, gpre, ((0,), (0,)))
        gbi_ref[...] += jnp.sum(gpre.astype(F32), axis=0, keepdims=True)
        return 0

    lax.fori_loop(0, total // tile, grads, 0)

    own_sends(False)
    first_step(False)
    lax.fori_loop(1, depth, lambda t, _: (later_step(t, False), 0)[1], 0)
    for copy in w_out_copies + w_relays:
        copy.wait_send()


def no_slope(n, rows, tile, a_chunk, *refs):
    return kernel(n, rows, tile, a_chunk, *refs[:16], None, *refs[16:])


def hand_out(*arrays):
    count = len(arrays)

    def copy_all(*refs):
        sems = refs[-1]
        copies = [
            pltpu.make_async_copy(refs[i], refs[count + i], sems.at[i])
            for i in range(count)
        ]
        for copy in copies:
            copy.start()
        for copy in copies:
            copy.wait()

    return pl.pallas_call(
        copy_all,
        out_shape=[jax.ShapeDtypeStruct(a.shape, a.dtype) for a in arrays],
        in_specs=[pl.BlockSpec(memory_space=pltpu.VMEM)] * count,
        out_specs=[pl.BlockSpec(memory_space=pl.ANY)] * count,
        scratch_shapes=[pltpu.SemaphoreType.DMA((count,))],
        compiler_params=pltpu.CompilerParams(vmem_limit_bytes=2 ** 20),
    )(*arrays)


def on_device(features, w_in, b_in, w_out, partner, window):
    n = lax.axis_size("dp")
    rows, chan = features.shape
    half = w_in.shape[1]
    embed = w_out.shape[1]
    total = n * rows
    tile = 4 * rows if n % 4 == 0 else rows
    anchors = n * A_DEV
    a_chunk = 256
    while a_chunk > A_DEV and (a_chunk * total > 2 ** 19 or anchors % a_chunk):
        a_chunk //= 2
    keep = total * half <= 2 ** 20
    scratch = [
        pltpu.VMEM((n * (rows + PAD), chan), BF16),
        pltpu.VMEM((n, 1, rows), jnp.int32),
        pltpu.VMEM((chan, half), BF16),
        pltpu.VMEM((1, half), F32),
        pltpu.VMEM((half, embed), BF16),
        pltpu.VMEM((total, half), BF16),
    ]
    if keep:
        scratch.append(pltpu.VMEM((total, half), F32))
    scratch += [
        pltpu.VMEM((total, embed), F32),
        pltpu.VMEM((total, embed), BF16),
        pltpu.VMEM((anchors, embed), BF16),
        pltpu.VMEM((anchors, embed), jnp.int32),
        pltpu.VMEM((a_chunk, total), F32),
        pltpu.VMEM((total, embed), F32),
        pltpu.SemaphoreType.DMA((4 * n,)),
        pltpu.SemaphoreType.DMA((n,)),
        pltpu.SemaphoreType.DMA((5,)),
        pltpu.SemaphoreType.DMA((5,)),
        pltpu.SemaphoreType.DMA((1,)),
    ]
    vmem = pl.BlockSpec(memory_space=pltpu.VMEM)
    loss, gwi, gbi, gwo = pl.pallas_call(
        functools.partial(kernel if keep else no_slope, n, rows, tile, a_chunk),
        out_shape=(
            pltpu.VMEM((1, A_DEV), F32),
            pltpu.VMEM((chan, half), F32),
            pltpu.VMEM((1, half), F32),
            pltpu.VMEM((half, embed), F32),
        ),
        in_specs=[vmem] * 5 + [pl.BlockSpec(memory_space=pltpu.SMEM)],
        out_specs=(vmem,) * 4,
        scratch_shapes=scratch,
        compiler_params=pltpu.CompilerParams(
            collective_id=0, has_side_effects=True, vmem_limit_bytes=64 * 2 ** 20 - 3 * 2 ** 20
        ),
    )(features, w_in, b_in.reshape(1, half), w_out, partner.reshape(1, rows), window)
    loss, gwi, gbi, gwo = hand_out(loss, gwi, gbi, gwo)
    return (loss.reshape(A_DEV), gwi, gbi.reshape(half), gwo)


def solution(mesh):
    return jax.shard_map(
        on_device,
        mesh=mesh,
        in_specs=(P("dp", None), P(None, "mp"), P("mp"), P("mp", None), P("dp"), P()),
        out_specs=(P("dp"), P(None, "mp"), P("mp"), P("mp", None)),
        check_vma=False,
    )
```

```python
import functools

import jax
import jax.numpy as jnp
from jax import lax
from jax.experimental import pallas as pl
from jax.experimental.pallas import tpu as pltpu
from jax.sharding import PartitionSpec as P

A_DEV = 32
PAD = 16
INV_TEMP = 10.0
SHIFT = 10.0
EPS = 1e-06
LOG2E = 1.4426950408889634
MESH = pl.DeviceIdType.MESH
F32 = jnp.float32
BF16 = jnp.bfloat16


def dot(a, b, dims=((1,), (0,))):
    return lax.dot_general(a, b, (dims, ((), ())), preferred_element_type=F32)


def kernel(
    n, rows, tile, a_chunk,
    f_ref, wi_ref, bi_ref, wo_ref, part_ref, win_ref,
    loss_ref, gwi_ref, gbi_ref, gwo_ref,
    feat, part, wi2, bi2, wo2, hid, dsil, proj, emb, anch, ids, ex, gemb,
    send_sem, recv_sem, w_send, w_recv, loc_sem,
):
    me = lax.axis_index("dp")
    other = 1 - lax.axis_index("mp")
    total = n * rows
    embed = wo_ref.shape[1]
    anchors = n * A_DEV
    chan, half = wi_ref.shape

    depth = n // 4
    z = me // 4
    x_at = lax.rem(me // 2, 2)
    core = lax.rem(me, 2)
    links = (me - 4, me + 4, me + 2 - 4 * x_at, me + 1 - 2 * core)
    LEFT, RIGHT, ACROSS, SIBLING = range(4)
    has_left = z > 0
    has_right = z < depth - 1

    barrier = pltpu.get_barrier_semaphore()

    def greet(where):
        pl.semaphore_signal(barrier, inc=1, device_id=where, device_id_type=MESH)

    greet({"mp": other})
    greet({"dp": links[ACROSS]})
    greet({"dp": links[SIBLING]})

    @pl.when(has_left)
    def _():
        greet({"dp": links[LEFT]})

    @pl.when(has_right)
    def _():
        greet({"dp": links[RIGHT]})

    slot_rows = rows + PAD
    own_f = pltpu.make_async_copy(
        f_ref, feat.at[pl.ds(me * slot_rows, rows)], loc_sem.at[0]
    )
    own_f.start()
    ints = part_ref[...]
    pair = jnp.concatenate([ints // rows, lax.rem(ints, rows)], axis=1).astype(F32)
    feat[pl.ds(pl.multiple_of(me * slot_rows + rows, PAD), PAD), 0:2 * rows] = (
        jnp.broadcast_to(pair, (PAD, 2 * rows)).astype(BF16)
    )
    pl.semaphore_wait(
        barrier, 3 + jnp.where(has_left, 1, 0) + jnp.where(has_right, 1, 0)
    )

    def item(slot, dest):
        ref = feat.at[pl.ds(slot * slot_rows, slot_rows)]
        return pltpu.make_async_remote_copy(
            src_ref=ref, dst_ref=ref,
            send_sem=send_sem.at[dest * n + slot], recv_sem=recv_sem.at[slot],
            device_id={"dp": links[dest]}, device_id_type=MESH,
        )

    def got(slot):
        item(slot, SIBLING).wait_recv()

    wi_cut, wo_cut = chan // 2, half // 2

    def weights(base, device, relay, c):
        wi_at = pl.ds(c * wi_cut, wi_cut)
        wo_at = pl.ds(c * wo_cut, wo_cut)
        pairs = [
            ((wi2 if relay else wi_ref).at[wi_at], wi2.at[wi_at]),
            ((wo2 if relay else wo_ref).at[wo_at], wo2.at[wo_at]),
        ]
        if not relay:
            pairs.append((bi_ref, bi2))
        return [
            pltpu.make_async_remote_copy(
                src_ref=src, dst_ref=dst, send_sem=w_send.at[base + i],
                recv_sem=w_recv.at[base + i], device_id=device, device_id_type=MESH,
            )
            for i, (src, dst) in enumerate(pairs)
        ]

    w_out_copies = weights(0, {"mp": other}, False, core)
    w_relays = weights(3, {"dp": links[SIBLING]}, True, core)
    w_from_sib = weights(3, {"dp": links[SIBLING]}, True, 1 - core)

    def to(slot, dest, start):
        if start:
            item(slot, dest).start()
        else:
            item(slot, dest).wait_send()

    def sides(slot, start):
        @pl.when(has_left)
        def _():
            to(slot, LEFT, start)

        @pl.when(has_right)
        def _():
            to(slot, RIGHT, start)

    along = core == 0
    twin_off = links[ACROSS] - me

    def own_sends(start):
        to(me, ACROSS, start)
        sides(me, start)
        to(me, SIBLING, start)

    def first_step(start):
        slot = me + twin_off
        if start:
            got(slot)

        @pl.when(core == 1)
        def _():
            sides(slot, start)

        to(slot, SIBLING, start)

    def from_side(slot, dest, more, start):
        if start:
            got(slot)

        @pl.when(more)
        def _():
            to(slot, dest, start)

        @pl.when(along)
        def _():
            to(slot, ACROSS, start)

        to(slot, SIBLING, start)

    def twin_of(slot, dest, more, start):
        twin = slot + twin_off
        if start:
            got(twin)

        @pl.when(more & (core == 1))
        def _():
            to(twin, dest, start)

        to(twin, SIBLING, start)

    def later_step(t, start):
        for each in (from_side, twin_of):
            @pl.when(z - t >= 0)
            def _():
                each(me - 4 * t, RIGHT, has_right, start)

            @pl.when(z + t < depth)
            def _():
                each(me + 4 * t, LEFT, has_left, start)

    def feat_rows(first, count):
        pieces = [
            feat[pl.ds(pl.multiple_of((first + i) * slot_rows, PAD), rows), :]
            for i in range(count)
        ]
        return jnp.concatenate(pieces, axis=0)

    def embed_chip(chip):
        first = chip * 2
        at = pl.ds(pl.multiple_of(first * rows, 2 * rows), 2 * rows)
        x = feat_rows(first, 2)
        pre = dot(x, wi_ref[...]) + bi_ref[...]
        sig = jax.nn.sigmoid(pre)
        h = (pre * sig).astype(BF16)
        hid[at, :] = h
        if dsil is not None:
            dsil[at, :] = sig * (1.0 + pre * (1.0 - sig))
        pre2 = dot(x, wi2[...]) + bi2[...]
        h2 = (pre2 * jax.nn.sigmoid(pre2)).astype(BF16)
        y = dot(h, wo_ref[...]) + dot(h2, wo2[...])
        proj[at, :] = y
        inv = lax.rsqrt(jnp.sum(y * y, axis=1, keepdims=True) + EPS)
        emb[at, :] = (y * inv).astype(BF16)
        gemb[at, :] = jnp.zeros((2 * rows, embed), F32)

    own_f.wait()
    own_sends(True)
    for copy in w_out_copies:
        copy.start()
    first_step(True)
    for copy in w_out_copies:
        copy.wait_recv()
    for copy in w_relays:
        copy.start()

    def gather_step(t, _):
        @pl.when(t < depth)
        def _():
            later_step(t, True)

        @pl.when(t == 1)
        def _():
            for copy in w_from_sib:
                copy.wait_recv()

        def one(j, _):
            step = t - 1
            z_from = jnp.where(j < 2, z - step, z + step)
            chip = z_from * 2 + lax.rem(j, 2)
            ok = (z_from >= 0) & (z_from < depth) & ((j < 2) | (step > 0))

            @pl.when(ok)
            def _():
                got(chip * 2 + 1 - core)
                embed_chip(chip)

            return 0

        lax.fori_loop(0, 4, one, 0)
        return 0

    lax.fori_loop(1, depth + 1, gather_step, 0)

    def window_of(b):
        return jnp.full((A_DEV, embed), win_ref[b], jnp.int32)

    def gather(b, _):
        win = window_of(b)
        picked = jnp.zeros((A_DEV, embed), F32)
        for w in range(rows // A_DEV):
            at = pl.ds(pl.multiple_of(b * rows + w * A_DEV, A_DEV), A_DEV)
            picked = jnp.where(win == w, emb[at, :].astype(F32), picked)
        at = pl.ds(pl.multiple_of(b * A_DEV, A_DEV), A_DEV)
        anch[at, :] = picked.astype(BF16)
        first = b * rows + win * A_DEV
        ids[at, :] = first + lax.broadcasted_iota(jnp.int32, (A_DEV, embed), 0)
        return 0

    lax.fori_loop(0, n, gather, 0, unroll=4)

    blocks = tile // rows
    reps = tile // embed

    def ids_of(base, size):
        return jnp.tile(ids[pl.ds(base, size), :], (1, reps))

    def col_ids(start, size):
        return start + lax.broadcasted_iota(jnp.int32, (size, tile), 1)

    def unpack(t, _):
        r = feat[pl.ds(pl.multiple_of(t * slot_rows + rows, PAD), PAD), 0:2 * rows]
        v = r.astype(F32).astype(jnp.int32)
        part[t] = v[0:1, :rows] * rows + v[0:1, rows:]
        return 0

    lax.fori_loop(0, n, unpack, 0, unroll=4)

    def part_row(t):
        pieces = [part[t * blocks + i] for i in range(blocks)]
        return jnp.concatenate(pieces, axis=1) if blocks > 1 else pieces[0]

    mine = pl.multiple_of(me * A_DEV, A_DEV)
    own_anch = anch[pl.ds(mine, A_DEV), :]
    own_ids = ids_of(mine, A_DEV)

    def own_tile(t, carry):
        tot, hit = carry
        start = pl.multiple_of(t * tile, tile)
        d = dot(own_anch, emb[pl.ds(start, tile), :], ((1,), (1,)))
        e = jnp.where(
            col_ids(start, A_DEV) == own_ids, 0.0,
            jnp.exp2(d * (INV_TEMP * LOG2E) - SHIFT * LOG2E),
        )
        tot = tot + jnp.sum(e, axis=1, keepdims=True)
        h = jnp.where(part_row(t) == own_ids, d, 0.0)
        return (tot, hit + jnp.sum(h, axis=1, keepdims=True))

    zero = jnp.zeros((A_DEV, 1), F32)
    tot, hit = lax.fori_loop(
        0, total // tile, own_tile, (zero, zero), unroll=total // tile <= 4
    )
    loss = jnp.log(tot) + SHIFT - hit * INV_TEMP
    r_iota = lax.broadcasted_iota(jnp.int32, (A_DEV, A_DEV), 0)
    c_iota = lax.broadcasted_iota(jnp.int32, (A_DEV, A_DEV), 1)
    loss_ref[...] = jnp.sum(jnp.where(r_iota == c_iota, loss, 0.0), axis=0, keepdims=True)

    few = total // tile <= 4

    def loss_chunk(k, _):
        base = pl.multiple_of(k * a_chunk, a_chunk)
        anc = anch[pl.ds(base, a_chunk), :]
        a_ids = ids_of(base, a_chunk)

        def soft(t, tot):
            start = pl.multiple_of(t * tile, tile)
            d = dot(anc, emb[pl.ds(start, tile), :], ((1,), (1,)))
            e = jnp.where(
                col_ids(start, a_chunk) == a_ids, 0.0,
                jnp.exp2(d * (INV_TEMP * LOG2E) - SHIFT * LOG2E),
            )
            ex[:, pl.ds(start, tile)] = e
            return tot + jnp.sum(e, axis=1, keepdims=True)

        tot = lax.fori_loop(0, total // tile, soft, jnp.zeros((a_chunk, 1), F32), unroll=few)
        inv = 1.0 / tot

        def back(t, acc):
            start = pl.multiple_of(t * tile, tile)
            at = pl.ds(start, tile)
            onehot = jnp.where(part_row(t) == a_ids, 1.0, 0.0)
            w = (ex[:, at] * inv - onehot).astype(BF16)
            gemb[at, :] += dot(w, anc, ((0,), (0,)))
            return acc + dot(w, emb[at, :])

        row = lax.fori_loop(
            0, total // tile, back, jnp.zeros((a_chunk, embed), F32), unroll=few
        )
        for i in range(a_chunk // A_DEV):
            b = k * (a_chunk // A_DEV) + i
            piece = row[i * A_DEV:(i + 1) * A_DEV, :]
            win = window_of(b)
            for w in range(rows // A_DEV):
                at = pl.ds(pl.multiple_of(b * rows + w * A_DEV, A_DEV), A_DEV)
                gemb[at, :] += jnp.where(win == w, piece, 0.0)
        return 0

    lax.fori_loop(0, anchors // a_chunk, loss_chunk, 0)

    gwi_ref[...] = jnp.zeros_like(gwi_ref)
    gwo_ref[...] = jnp.zeros_like(gwo_ref)
    gbi_ref[...] = jnp.zeros_like(gbi_ref)

    def grads(t, _):
        at = pl.ds(pl.multiple_of(t * tile, tile), tile)
        y = proj[at, :]
        inv = lax.rsqrt(jnp.sum(y * y, axis=1, keepdims=True) + EPS)
        unit = y * inv
        g = gemb[at, :] * (INV_TEMP / anchors)
        gp = ((g - unit * jnp.sum(unit * g, axis=1, keepdims=True)) * inv).astype(BF16)
        x = feat_rows(t * blocks, blocks)
        h = hid[at, :]
        gwo_ref[...] += dot(h, gp, ((0,), (0,)))
        if dsil is not None:
            slope = dsil[at, :]
        else:
            pre = dot(x, wi_ref[...]) + bi_ref[...]
            sig = jax.nn.sigmoid(pre)
            slope = sig * (1.0 + pre * (1.0 - sig))
        gpre = (dot(gp, wo_ref[...], ((1,), (1,))) * slope).astype(BF16)
        gwi_ref[...] += dot(x, gpre, ((0,), (0,)))
        gbi_ref[...] += jnp.sum(gpre.astype(F32), axis=0, keepdims=True)
        return 0

    lax.fori_loop(0, total // tile, grads, 0, unroll=few)

    own_sends(False)
    first_step(False)
    lax.fori_loop(1, depth, lambda t, _: (later_step(t, False), 0)[1], 0)
    for copy in w_out_copies + w_relays:
        copy.wait_send()


def no_slope(n, rows, tile, a_chunk, *refs):
    return kernel(n, rows, tile, a_chunk, *refs[:16], None, *refs[16:])


def hand_out(*arrays):
    count = len(arrays)

    def copy_all(*refs):
        sems = refs[-1]
        copies = [
            pltpu.make_async_copy(refs[i], refs[count + i], sems.at[i])
            for i in range(count)
        ]
        for copy in copies:
            copy.start()
        for copy in copies:
            copy.wait()

    return pl.pallas_call(
        copy_all,
        out_shape=[jax.ShapeDtypeStruct(a.shape, a.dtype) for a in arrays],
        in_specs=[pl.BlockSpec(memory_space=pltpu.VMEM)] * count,
        out_specs=[pl.BlockSpec(memory_space=pl.ANY)] * count,
        scratch_shapes=[pltpu.SemaphoreType.DMA((count,))],
        compiler_params=pltpu.CompilerParams(vmem_limit_bytes=2 ** 20),
    )(*arrays)


def on_device(features, w_in, b_in, w_out, partner, window):
    n = lax.axis_size("dp")
    rows, chan = features.shape
    half = w_in.shape[1]
    embed = w_out.shape[1]
    total = n * rows
    tile = 4 * rows if n % 4 == 0 else rows
    anchors = n * A_DEV
    a_chunk = 256
    while a_chunk > A_DEV and (a_chunk * total > 2 ** 19 or anchors % a_chunk):
        a_chunk //= 2
    keep = total * half <= 2 ** 20
    scratch = [
        pltpu.VMEM((n * (rows + PAD), chan), BF16),
        pltpu.VMEM((n, 1, rows), jnp.int32),
        pltpu.VMEM((chan, half), BF16),
        pltpu.VMEM((1, half), F32),
        pltpu.VMEM((half, embed), BF16),
        pltpu.VMEM((total, half), BF16),
    ]
    if keep:
        scratch.append(pltpu.VMEM((total, half), F32))
    scratch += [
        pltpu.VMEM((total, embed), F32),
        pltpu.VMEM((total, embed), BF16),
        pltpu.VMEM((anchors, embed), BF16),
        pltpu.VMEM((anchors, embed), jnp.int32),
        pltpu.VMEM((a_chunk, total), F32),
        pltpu.VMEM((total, embed), F32),
        pltpu.SemaphoreType.DMA((4 * n,)),
        pltpu.SemaphoreType.DMA((n,)),
        pltpu.SemaphoreType.DMA((5,)),
        pltpu.SemaphoreType.DMA((5,)),
        pltpu.SemaphoreType.DMA((1,)),
    ]
    vmem = pl.BlockSpec(memory_space=pltpu.VMEM)
    loss, gwi, gbi, gwo = pl.pallas_call(
        functools.partial(kernel if keep else no_slope, n, rows, tile, a_chunk),
        out_shape=(
            pltpu.VMEM((1, A_DEV), F32),
            pltpu.VMEM((chan, half), F32),
            pltpu.VMEM((1, half), F32),
            pltpu.VMEM((half, embed), F32),
        ),
        in_specs=[vmem] * 5 + [pl.BlockSpec(memory_space=pltpu.SMEM)],
        out_specs=(vmem,) * 4,
        scratch_shapes=scratch,
        compiler_params=pltpu.CompilerParams(
            collective_id=0, has_side_effects=True, vmem_limit_bytes=64 * 2 ** 20 - 3 * 2 ** 20
        ),
    )(features, w_in, b_in.reshape(1, half), w_out, partner.reshape(1, rows), window)
    loss, gwi, gbi, gwo = hand_out(loss, gwi, gbi, gwo)
    return (loss.reshape(A_DEV), gwi, gbi.reshape(half), gwo)


def solution(mesh):
    return jax.shard_map(
        on_device,
        mesh=mesh,
        in_specs=(P("dp", None), P(None, "mp"), P("mp"), P("mp", None), P("dp"), P()),
        out_specs=(P("dp"), P(None, "mp"), P("mp"), P("mp", None)),
        check_vma=False,
    )
```
